32 devices in a mesh: dp: 4 (over y, x), tensor: 8 (over z, core).
Axes of the slice: x: 2, y: 2, z: 4, core: 2. Of those that a mesh axis runs over, the one named last changes fastest.
Arguments:
- calibration: bfloat16 [1024, 6144], P('dp'), may hold values from -60 to 60
- expert_ids: int32 [1024, 2], P('dp'), may hold values from 0 to 7, all different within a row; in each aligned block of 256 rows (0 to 255, 256 to 511, ...) at most 80 rows name the same one
- chosen_expert: int32 [1], replicated, may hold values from 0 to 7
- ratio_ids: int32 [10], replicated, may hold values from 0 to 19
- gate_weight: bfloat16 [6144, 16384], P('dp', 'tensor'), may hold values from -0.078125 to 0.078125
Outputs:
- col_loss: float32 [10, 16384], P(None, 'tensor')
- losses: float32 [10], replicated
- best_loss: float32 [1], replicated
The draws below stay inside these ranges and needn't reach their ends.
Inputs may be any that keep to these rules, and one draw needn't show every extreme that they name: `expert_ids`: each row names two different experts; in the rows of one device no expert is named by more than 80 rows, a bound that some block reaches; every expert is named by some row.
All inputs are finite; a program needn't handle non-finite values.
Results may differ from the reference program's by a relative error of at most 0.0044.
Values may be sent and summed in bfloat16 or wider, within the bound.
No kernel may reach another device: no remote copies, remote signals or barrier semaphores. Data moves between devices by JAX's collectives and lax.ppermute only.
A program may use at most 128 MiB of HBM per device.

```python
import math
import jax
import jax.numpy as jnp
import numpy as np
from jax import lax

D = 6144
FF = 16384
EXPERTS = 8
TOK_DEV = 256
RATIOS = 10
GRID = 20
GROUP = 128
CAP = 80
TOKENS = 1024
N_DP = 4


def draw_calibration(key, part):
    first, second = jax.random.split(key, 2)
    channel_scale = jnp.exp(jax.random.uniform(first, (D,), jnp.float32, -2.0, 2.0))
    values = jnp.clip(jax.random.normal(second, (TOKENS, D), jnp.float32), -6.0, 6.0)
    return (values * channel_scale[None, :]).astype(jnp.bfloat16)


def touch_ends(result, rng, low, largest):
    longest = result.shape.index(max(result.shape))
    spots = []
    for shift in (0, 1):
        where = [jax.random.randint(jax.random.fold_in(rng, axis), (), 0, length) for axis, length in enumerate(result.shape)]
        where[longest] = (where[longest] + shift) % result.shape[longest]
        spots.append(tuple(where))
    return result.at[spots[0]].set(low).at[spots[1]].set(largest)


def steps_of(rng, dims, cuts, low, high):
    loudness, own = 1.0, jax.random.fold_in(rng, 6)
    for dim, blocks in cuts:
        heights = jnp.exp(jax.random.uniform(jax.random.fold_in(own, dim), (blocks,), jnp.float32, low / len(cuts), high / len(cuts)))
        loudness = loudness * jnp.repeat(heights, dims[dim] // blocks).reshape([-1 if axis == dim else 1 for axis in range(len(dims))])
    return loudness


def assign_block(stream_key, own, number, rows, count, top, most, skew):
    ranking = jax.random.permutation(stream_key, count)
    crowded, ordinary = portions_of(count, rows * top, most, skew, True), portions_of(count, rows * top, most, skew, False)
    places = jnp.arange(count)

    def named(lengths, turn):
        used = int((lengths > 0).sum())
        fixed = max(1, used // 4)
        passed = fixed + (places - fixed + turn * (used - fixed)) % max(1, count - fixed)
        return jnp.zeros((count,), jnp.int32).at[ranking[jnp.where(places < fixed, places, passed)]].set(jnp.asarray(lengths, jnp.int32))

    lengths = jnp.where(number % 4 == 0, named(crowded, number // 4), named(ordinary, number - number // 4 - 1))
    mixed = jax.random.permutation(jax.random.fold_in(own, 3), count)
    source_of, receiver = mixed[0:count // 2 * 2:2], mixed[1:count // 2 * 2:2]
    room = jnp.minimum(lengths[source_of] - 1, most - lengths[receiver]) // 2
    room = jnp.where((source_of == ranking[0]) | (receiver == ranking[0]) | (lengths[receiver] == 0), 0, jnp.maximum(room, 0))
    passed = jax.random.randint(jax.random.fold_in(own, 4), (count // 2,), 0, 1 << 20) % (room + 1)
    lengths = lengths.at[source_of].add(-passed).at[receiver].add(passed)
    items = jnp.searchsorted(jnp.cumsum(lengths), jnp.arange(rows * top), side="right").astype(jnp.int32)
    grid = items.reshape(top, rows).T
    grid = grid[jax.random.permutation(jax.random.fold_in(own, 1), rows)]
    turn = jax.random.randint(jax.random.fold_in(own, 2), (rows, 1), 0, top)
    return jnp.take_along_axis(grid, (jnp.arange(top)[None, :] + turn) % top, axis=1)


def portions_of(number_of, total, most, lean, full):
    portions = [(1 << 20) // math.isqrt(standing ** lean) + 1 for standing in range(1, number_of + 1)]
    largest = most if full else min(most, max(-(-total // number_of), total * portions[0] // sum(portions)))
    least = 1 if total - largest >= number_of - 1 else 0
    counts, spare = [largest] + [least] * (number_of - 1), total - largest - least * (number_of - 1)
    while spare > 0:
        movable = [i for i in range(1, number_of) if counts[i] < largest] or [i for i in range(1, number_of) if counts[i] < most]
        mass, remaining = sum([portions[i] for i in movable]), spare
        for i in movable:
            extra = min(most - counts[i], max(1, remaining * portions[i] // mass), spare)
            counts[i] = counts[i] + extra
            spare = spare - extra
    return np.array(counts)


def noise(own_key, extent, width, most, shards=(), held_as=jnp.bfloat16):
    factor_of = steps_of(own_key, extent, shards, -0.22, 0.18) if shards else 1.0
    drawn = jax.random.normal(own_key, extent, jnp.float32) * width * factor_of
    return jnp.minimum(jnp.maximum(drawn, -most), most).astype(held_as)


def setup_inputs(seed: int = 0) -> dict:
    arg_keys = jax.random.split(jax.random.key(seed), 6)
    calibration = draw_calibration(jax.random.fold_in(arg_keys[5], 71), 0)
    expert_ids_keys = jax.random.split(jax.random.fold_in(arg_keys[1], 1), TOKENS // TOK_DEV)
    expert_ids_turns = jax.random.permutation(jax.random.fold_in(arg_keys[1], 3), TOKENS // TOK_DEV)
    expert_ids = jax.vmap(lambda own, number: assign_block(jax.random.fold_in(arg_keys[1], 2), own, number, TOK_DEV, EXPERTS, 2, CAP, 1))(expert_ids_keys, expert_ids_turns).reshape((TOKENS, 2))
    chosen_expert = jax.random.randint(arg_keys[2], (1,), 0, EXPERTS).astype(jnp.int32)
    ratio_ids = touch_ends(jax.random.randint(arg_keys[3], (RATIOS,), 0, GRID), jax.random.fold_in(arg_keys[3], 1), 0, GRID - 1).astype(jnp.int32)
    gate_weight = noise(arg_keys[4], (D, FF), D ** -0.5, 0.078125, ((0, 4), (1, 8)))
    return dict(calibration=calibration, expert_ids=expert_ids, chosen_expert=chosen_expert, ratio_ids=ratio_ids, gate_weight=gate_weight)


LEVELS = 7.0
LOSS_SCALE = 100.0


def pick_rows(expert_rows, block, expert, capacity):
    hit = jnp.any(expert_rows == expert, axis=1)
    position = jnp.cumsum(hit.astype(jnp.int32)) - 1
    slots = jnp.arange(capacity, dtype=jnp.int32)
    selected = hit[None, :] & (position[None, :] == slots[:, None])
    order = jnp.arange(block.shape[0], dtype=jnp.int32)
    row_index = jnp.sum(jnp.where(selected, order[None, :], 0), axis=1).astype(jnp.int32)
    occupied = jnp.any(selected, axis=1)
    routed = jnp.where(occupied[:, None], jnp.take(block, row_index, axis=0), jnp.zeros((), block.dtype))
    return routed, occupied


def error_matrix(weight, channel_sum, ratio):
    exponent = ratio.astype(jnp.float32) / GRID
    scales = jnp.exp(exponent * jnp.log(channel_sum))
    scaled = weight.astype(jnp.float32) * scales[:, None]
    grouped = scaled.reshape(weight.shape[0] // GROUP, GROUP, weight.shape[1])
    step_size = (jnp.max(jnp.abs(grouped), axis=1) + 1e-6) / LEVELS
    phase = grouped / step_size[:, None, :]
    error = (-step_size[:, None, :] / (2.0 * math.pi)) * jnp.sin(2.0 * math.pi * phase)
    return (error.reshape(weight.shape) / scales[:, None]).astype(jnp.bfloat16)


def reference(calibration, expert_ids, chosen_expert, ratio_ids, gate_weight):
    blocks = calibration.reshape(N_DP, TOK_DEV, D)
    id_blocks = expert_ids.reshape(N_DP, TOK_DEV, 2)
    routed, occupied = jax.vmap(lambda ids, block: pick_rows(ids, block, chosen_expert[0], CAP))(id_blocks, blocks)
    routed = routed.reshape(N_DP * CAP, D)
    token_count = jnp.sum(occupied.astype(jnp.float32))
    channel_sum = 0.001 + jnp.sum(jnp.abs(routed.astype(jnp.float32)), axis=0)
    routed_wide = routed.astype(jnp.float32)

    def per_ratio(ratio):
        error = error_matrix(gate_weight, channel_sum, ratio)
        product = jnp.dot(routed_wide, error.astype(jnp.float32))
        return LOSS_SCALE * jnp.sum(product * product, axis=0) / token_count

    col_loss = lax.map(per_ratio, ratio_ids)
    losses = jnp.sum(col_loss, axis=1) / FF
    best_loss = jnp.min(losses)[None]
    return col_loss, losses, best_loss
```

```python
import functools
import math

import jax
import jax.numpy as jnp
from jax import lax
from jax.experimental import pallas as pl
from jax.experimental.pallas import tpu as pltpu
from jax.sharding import PartitionSpec as P

FF = 16384
GRID = 20
GROUP = 128
CAP = 80
LEVELS = 7.0
LOSS_SCALE = 100.0
TILE = 256
RPAD = 16
SINE = (12.56674999, 50.15085936, 76.37654413)


def route_kernel(chosen, ids_ref, calib_ref, routed_ref, sums_ref, sel_ref):
    tokens = calib_ref.shape[0]

    @pl.when(pl.program_id(0) == 0)
    def _():
        ids = ids_ref[...]
        hit = jnp.max(jnp.where(ids == chosen[0], 1.0, 0.0), axis=0, keepdims=True)
        row = lax.broadcasted_iota(jnp.int32, (tokens, tokens), 0)
        col = lax.broadcasted_iota(jnp.int32, (tokens, tokens), 1)
        upto = jnp.where(row <= col, 1.0, 0.0).astype(jnp.bfloat16)
        hits = jnp.broadcast_to(hit, (16, tokens)).astype(jnp.bfloat16)
        place = jnp.dot(hits, upto, preferred_element_type=jnp.float32)[:1]
        place = jnp.where(hit > 0.0, place, 0.0)
        slot = lax.broadcasted_iota(jnp.int32, (CAP, tokens), 0).astype(jnp.float32) + 1.0
        sel_ref[...] = jnp.where(slot == place, 1.0, 0.0).astype(jnp.bfloat16)

    picked = jnp.dot(sel_ref[...], calib_ref[...], preferred_element_type=jnp.float32)
    routed_ref[...] = picked.astype(jnp.bfloat16)
    sums_ref[...] = jnp.sum(jnp.abs(picked), axis=0, keepdims=True)


def route(calibration, expert_ids, chosen):
    tokens, width = calibration.shape
    step = width // 6 if width % (6 * 128) == 0 else width
    ids = jnp.pad(expert_ids.T, ((0, 6), (0, 0)), constant_values=-1)
    return pl.pallas_call(
        route_kernel,
        out_shape=(
            jax.ShapeDtypeStruct((CAP, width), jnp.bfloat16),
            jax.ShapeDtypeStruct((1, width), jnp.float32),
        ),
        grid_spec=pltpu.PrefetchScalarGridSpec(
            num_scalar_prefetch=1,
            grid=(width // step,),
            in_specs=[
                pl.BlockSpec((8, tokens), lambda i, c: (0, 0)),
                pl.BlockSpec((tokens, step), lambda i, c: (0, i)),
            ],
            out_specs=(
                pl.BlockSpec((CAP, step), lambda i, c: (0, i)),
                pl.BlockSpec((1, step), lambda i, c: (0, i)),
            ),
            scratch_shapes=[pltpu.VMEM((CAP, tokens), jnp.bfloat16)],
        ),
        name="route",
    )(chosen, ids, calibration)


def block_kernel(first, last, chunk, where, w_ref, x_ref, s_ref, *rest):
    acc_ref = None if first else rest[0]
    out_ref, wide, err, scaled_x, s_col, s_wide = rest[-6:]
    rows, cols = w_ref.shape
    total = x_ref.shape[1]
    ratios = pl.num_programs(0) - 1
    step_id = pl.program_id(0)
    groups, halves = rows // GROUP, cols // TILE
    now = lax.rem(step_id, 2)
    prev = 1 - now
    lead = SINE[2]

    def spread(g, ratio, to):
        d = pl.ds(g * GROUP, GROUP)
        s_wide[to, d, :] = jnp.take_along_axis(
            s_col[d, :], jnp.full((GROUP, 128), ratio, jnp.int32), axis=1
        )

    @pl.when(step_id == 0)
    def _():
        for g in range(groups):
            d = pl.ds(g * GROUP, GROUP)
            wide[d, :] = w_ref[d, :].astype(jnp.float32)
            s_col[d, :RPAD] = s_ref[:, g * GROUP : (g + 1) * GROUP].T
            spread(g, 0, 0)

    def errors(tick):
        for g in range(groups):
            d = pl.ds(g * GROUP, GROUP)
            for c in range(halves):
                l = pl.ds(c * TILE, TILE)
                s = s_wide[now, d, :]
                scaled = wide[d, l] * jnp.concatenate([s] * (TILE // 128), axis=1)
                top = jnp.max(jnp.abs(scaled), axis=0, keepdims=True) + 1e-06
                inverse = LEVELS / top
                height = top * (-lead / (LEVELS * 2.0 * math.pi))
                for k in range(0, GROUP, chunk):
                    phase = scaled[k : k + chunk] * inverse
                    f = phase - jnp.round(phase)
                    v = f * (0.5 - jnp.abs(f))
                    u = jnp.abs(v)
                    q = (u + SINE[1] / lead) * u + SINE[0] / lead
                    err[now, pl.ds(g * GROUP + k, chunk), l] = ((v * height) * q).astype(jnp.bfloat16)
                    tick()
            spread(g, jnp.minimum(step_id + 1, ratios - 1), prev)

    def products(accs):
        todo = []
        depth = rows // TILE

        def push(k, n):
            pltpu.matmul_push_rhs(err[prev, pl.ds(k * TILE, TILE), pl.ds(n * TILE, TILE)], k % 2, n)

        def feed(k, n, t):
            pltpu.matmul_acc_lhs(
                accs[n][t],
                scaled_x[prev, pl.ds(t * CAP, CAP), pl.ds(k * TILE, TILE)],
                load_staged_rhs=k % 2 if t == 0 else None,
            )

        def pop(n, t, sums):
            l, rows_t = pl.ds(n * TILE, TILE), pl.ds(t * CAP, CAP)
            part = pltpu.matmul_pop(accs[n][t])
            if acc_ref is not None:
                part = part + acc_ref[0, rows_t, l]
            if last:
                sums[n] = sums[n] + jnp.sum(part * part, axis=0, keepdims=True)
                if (t + 1) * CAP == total:
                    out_ref[0, :, l] = sums[n]
            else:
                out_ref[0, rows_t, l] = part

        blocks = total // CAP
        todo += [functools.partial(push, 0, n) for n in range(halves)]
        for k in range(depth):
            for t in range(blocks):
                todo += [functools.partial(feed, k, n, t) for n in range(halves)]
                if t == 0 and k + 1 < depth:
                    todo += [functools.partial(push, k + 1, n) for n in range(halves)]
        sums = [0.0] * halves
        for t in range(blocks):
            todo += [functools.partial(pop, n, t, sums) for n in range(halves)]
        return todo

    def run(*accs):
        @pl.when(step_id < ratios)
        def _():
            inverse_s = 1.0 / s_ref[pl.ds(step_id, 1), :]
            scaled_x[now] = x_ref[0] * inverse_s.astype(jnp.bfloat16)
            todo = products(accs)
            ticks = groups * halves * (GROUP // chunk)
            state = [0, 0]

            def tick():
                state[0] += 1
                while state[1] < len(todo) * state[0] // ticks:
                    todo[state[1]]()
                    state[1] += 1

            errors(tick)

        @pl.when(step_id == ratios)
        def _():
            for task in products(accs):
                task()

    pl.run_scoped(run, *[[pltpu.ACC(n)((CAP, TILE), jnp.float32)] * (total // CAP) for n in range(halves)])


def block(weight, w_block, routed, x_block, scales, s_block, acc, ratios, rows, cols, last, chunk=32):
    total = routed.shape[1]
    first = acc is None
    once = pl.Buffered(1)
    ahead = lambda j, i: (jnp.maximum(j - 1, 0), 0, 0)
    acc_spec = pl.BlockSpec((1, total, cols), ahead)
    if last:
        out_shape, out_spec = (ratios, 1, cols), pl.BlockSpec((1, 1, cols), ahead)
    else:
        out_shape, out_spec = (ratios, total, cols), acc_spec
    w_row, w_col = w_block
    where = jnp.stack([jnp.int32(v) for v in (w_row, w_col, x_block[0], x_block[1], s_block)])
    in_specs = [
        pl.BlockSpec((rows, cols), lambda j, i: (i[0], i[1]), pipeline_mode=once),
        pl.BlockSpec((1, total, rows), lambda j, i: (i[2], 0, i[3]), pipeline_mode=once),
        pl.BlockSpec((RPAD, rows), lambda j, i: (0, i[4]), pipeline_mode=once),
    ]
    work = ratios * rows * cols
    return pl.pallas_call(
        functools.partial(block_kernel, first, last, chunk),
        out_shape=jax.ShapeDtypeStruct(out_shape, jnp.float32),
        grid_spec=pltpu.PrefetchScalarGridSpec(
            num_scalar_prefetch=1,
            grid=(ratios + 1,),
            in_specs=in_specs + ([] if first else [acc_spec]),
            out_specs=out_spec,
            scratch_shapes=[
                pltpu.VMEM((rows, cols), jnp.float32),
                pltpu.VMEM((2, rows, cols), jnp.bfloat16),
                pltpu.VMEM((2, total, rows), jnp.bfloat16),
                pltpu.VMEM((rows, 128), jnp.float32),
                pltpu.VMEM((2, rows, 128), jnp.float32),
            ],
        ),
        compiler_params=pltpu.CompilerParams(
            vmem_limit_bytes=48 * 1024 * 1024,
        ),
        cost_estimate=pl.CostEstimate(
            flops=2 * total * work, bytes_accessed=8 * ratios * total * cols, transcendentals=0
        ),
        name="search_block",
    )(where, weight, routed, scales, *([] if first else [acc]))


def swapped(value, axis, size, k):
    return lax.ppermute(value, axis, [(i, i ^ k) for i in range(size)])


def tree_sum(parts):
    while len(parts) > 1:
        parts = [a + b for a, b in zip(parts[::2], parts[1::2])]
    return parts[0]


def in_order(parts, me):
    bit = 1
    while bit < len(parts):
        swap = (me & bit) != 0
        parts = [jnp.where(swap, parts[i ^ bit], parts[i]) for i in range(len(parts))]
        bit *= 2
    return parts


def search(n_dp, n_tensor, calibration, expert_ids, chosen_expert, ratio_ids, gate_weight):
    me, column = lax.axis_index("dp"), lax.axis_index("tensor")
    half = column & 1
    rows, width = gate_weight.shape
    cols = width // n_dp
    ratios = ratio_ids.shape[0]
    model = calibration.shape[1]

    sent = {}
    for k in range(1, n_dp):
        piece = lax.dynamic_slice(gate_weight, (0, (me ^ k) * cols), (rows, cols))
        sent[k] = swapped(piece, "dp", n_dp, k)

    routed, sums = route(calibration, expert_ids, chosen_expert)
    count = jnp.sum(jnp.any(expert_ids == chosen_expert[0], axis=1).astype(jnp.float32))
    sums = jnp.concatenate([sums, jnp.full((1, 128), count)], axis=1)
    all_sums = tree_sum([sums] + [swapped(sums, "dp", n_dp, k) for k in range(1, n_dp)])
    channel_sum = 0.001 + all_sums[:, :model]
    token_count = all_sums[0, model]

    mine = lax.dynamic_slice(routed, (0, half * (model // 2)), (CAP, model // 2))
    mine = jnp.concatenate([mine] + [swapped(mine, "dp", n_dp, k) for k in range(1, n_dp)], axis=0)
    other = swapped(mine, "tensor", n_tensor, 1)
    everything = jnp.stack([mine, other])

    exponent = jnp.pad(ratio_ids.astype(jnp.float32) / GRID, (0, RPAD - ratios))
    scales = jnp.exp(exponent[:, None] * jnp.log(channel_sum))

    acc = None
    per_half = n_dp // 2
    for k in range(n_dp):
        b = me ^ k
        source, place = (gate_weight, (0, me)) if k == 0 else (sent[k], (0, 0))
        x_place = ((b // per_half) ^ half, b % per_half)
        acc = block(source, place, everything, x_place, scales, b, acc, ratios, rows, cols, k == n_dp - 1)

    piece = LOSS_SCALE * acc[:, 0] / token_count
    parts = [piece] + [swapped(piece, "dp", n_dp, k) for k in range(1, n_dp)]
    parts = in_order(parts, me)
    col_loss = jnp.concatenate(parts, axis=1)
    local = jnp.sum(col_loss, axis=1)
    losses = tree_sum([local] + [swapped(local, "tensor", n_tensor, k) for k in range(1, n_tensor)]) / FF
    return col_loss, losses, jnp.min(losses)[None]


def pick_rows(expert_rows, block, expert, capacity):
    hit = jnp.any(expert_rows == expert, axis=1)
    position = jnp.cumsum(hit.astype(jnp.int32)) - 1
    slots = jnp.arange(capacity, dtype=jnp.int32)
    selected = hit[None, :] & (position[None, :] == slots[:, None])
    order = jnp.arange(block.shape[0], dtype=jnp.int32)
    row_index = jnp.sum(jnp.where(selected, order[None, :], 0), axis=1)
    occupied = jnp.any(selected, axis=1)
    routed = jnp.where(
        occupied[:, None], jnp.take(block, row_index, axis=0), jnp.zeros((), block.dtype)
    )
    return (routed, occupied)


def error_matrix(weight, channel_sum, ratio):
    exponent = ratio.astype(jnp.float32) / GRID
    scales = jnp.exp(exponent * jnp.log(channel_sum))
    scaled = weight.astype(jnp.float32) * scales[:, None]
    grouped = scaled.reshape(weight.shape[0] // GROUP, GROUP, weight.shape[1])
    step_size = (jnp.max(jnp.abs(grouped), axis=1) + 1e-06) / LEVELS
    phase = grouped / step_size[:, None, :]
    error = -step_size[:, None, :] / (2.0 * math.pi) * jnp.sin(2.0 * math.pi * phase)
    return (error.reshape(weight.shape) / scales[:, None]).astype(jnp.bfloat16)


def body(calibration, expert_ids, chosen_expert, ratio_ids, gate_weight):
    routed, occupied = pick_rows(expert_ids, calibration, chosen_expert[0], CAP)
    gathered, marks = (
        lax.all_gather(routed, "dp", axis=0, tiled=True),
        lax.all_gather(occupied.astype(jnp.bfloat16), "dp", axis=0, tiled=True),
    )
    channel_sum = 0.001 + jnp.sum(jnp.abs(gathered.astype(jnp.float32)), axis=0)
    token_count = jnp.sum(marks.astype(jnp.float32))
    columns = lax.all_to_all(gate_weight, "dp", split_axis=1, concat_axis=0, tiled=True)
    errors = jax.vmap(lambda ratio: error_matrix(columns, channel_sum, ratio))(ratio_ids)
    product = jnp.einsum("td,rdc->rtc", gathered, errors, preferred_element_type=jnp.float32)
    piece = LOSS_SCALE * jnp.sum(product * product, axis=1) / token_count
    col_loss = lax.all_gather(piece, "dp", axis=1, tiled=True)
    losses = lax.psum(jnp.sum(col_loss, axis=1), "tensor") / FF
    best_loss = jnp.min(losses)[None]
    return (col_loss, losses, best_loss)


def solution(mesh):
    placed = (P("dp", None), P("dp", None), P(), P(), P("dp", "tensor"))
    n_dp, n_tensor = mesh.shape["dp"], mesh.shape["tensor"]

    def run(calibration, expert_ids, chosen_expert, ratio_ids, gate_weight):
        rows, width = gate_weight.shape
        cols = width // n_dp
        powers = n_dp & (n_dp - 1) == 0 and n_tensor & (n_tensor - 1) == 0
        tiled = rows % TILE == 0 and cols % TILE == 0 and cols // TILE <= 2 and n_dp * CAP <= 1024
        if powers and n_dp > 1 and n_tensor > 1 and tiled and ratio_ids.shape[0] <= RPAD:
            return search(n_dp, n_tensor, calibration, expert_ids, chosen_expert, ratio_ids, gate_weight)
        return body(calibration, expert_ids, chosen_expert, ratio_ids, gate_weight)

    return jax.shard_map(
        run, mesh=mesh, in_specs=placed, out_specs=(P(None, "tensor"), P(), P()), check_vma=False
    )
```
